32 devices in a mesh: tm: 8 (over z, x), dp: 4 (over y, core).
Axes of the slice: x: 2, y: 2, z: 4, core: 2. Of those that a mesh axis runs over, the one named last changes fastest.
Arguments:
- frames: bfloat16 [4, 1024, 1024], P('dp', 'tm'), may hold values from -6 to 6
- grad_frames: bfloat16 [4, 1024, 1024], P('dp', 'tm'), may hold values from -6 to 6
- w_qkv: bfloat16 [1024, 2304], replicated, may hold values from -0.1875 to 0.1875
- w_out: bfloat16 [1024, 768], replicated, may hold values from -0.21875 to 0.21875
Outputs:
- grad_input: bfloat16 [4, 1024, 1024], P('dp', 'tm')
- grad_qkv: float32 [1024, 2304], P('tm')
- grad_out: float32 [1024, 768], P('tm')
The draws below stay inside these ranges and needn't reach their ends.
All inputs are finite; a program needn't handle non-finite values.
Results may differ from the reference program's by a relative error of at most 0.014.
Values sent between devices are 32-bit elements; how exact they have to be, the bound alone decides.
A program may use at most 64 MiB of HBM per device.

```python
import jax
import jax.numpy as jnp
from jax import lax

D = 1024
HEADS = 12
HEAD = 64
HE = 768
BLOCK = 128
LEN = 1024
UTTS = 4


def raised(drawn, rng, source, target, shards_of, factor):
    def block_of(position):
        return (jnp.arange(drawn.shape[position]) // (drawn.shape[position] // shards_of)).reshape((-1,) + (1,) * (drawn.ndim - 1 - position))

    first = jax.random.permutation(rng, shards_of)[block_of(target)]
    other_side = (block_of(target) + shards_of // 2) % shards_of
    return jnp.where((block_of(source) == first) | (block_of(source) == other_side), factor * drawn, drawn)


def shard_levels(own_key, extent, shards, smallest, top_value):
    def one(position, blocks):
        draws = jax.random.uniform(jax.random.fold_in(jax.random.fold_in(own_key, 6), position), (blocks,), jnp.float32, smallest / len(shards), top_value / len(shards))
        return jnp.repeat(jnp.exp(draws), extent[position] // blocks).reshape((-1,) + (1,) * (len(extent) - position - 1))

    level = one(*shards[0])
    for cut in shards[1:]:
        level = level * one(*cut)
    return level


def gaussian(rng, dims, scale, limit, split=(), held_as=jnp.bfloat16):
    factor_of = shard_levels(rng, dims, split, -0.22, 0.18) if split else 1.0
    array = jax.random.normal(rng, dims, jnp.float32) * scale * factor_of
    return jnp.minimum(jnp.maximum(array, -limit), limit).astype(held_as)


def gaussian_with(key, shape, spread, reach, pieces, heavy, kind=jnp.bfloat16):
    drawn = spread * jax.random.normal(key, shape, jnp.float32)
    if pieces:
        drawn = drawn * shard_levels(key, shape, pieces, -0.22, 0.18)
    return jnp.clip(raised(drawn, jax.random.fold_in(key, 3), *heavy), -reach, reach).astype(kind)


def setup_inputs(seed: int = 0) -> dict:
    seeds = jax.random.split(jax.random.key(seed), 5)
    return {
        "frames": gaussian_with(seeds[0], (UTTS, LEN, D), 1.0, 6.0, ((0, 4), (1, 8)), (1, 2, 8, 2.0)),
        "grad_frames": gaussian_with(seeds[1], (UTTS, LEN, D), 1.0, 6.0, ((0, 4), (1, 8)), (1, 2, 8, 2.0)),
        "w_qkv": gaussian(seeds[2], (D, 3 * HE), D ** -0.5, 0.1875),
        "w_out": gaussian(seeds[3], (D, HE), HE ** -0.5, 0.21875),
    }


def features(a):
    return jnp.where(a > 0, a + 1.0, jnp.exp(jnp.minimum(a, 0.0)))


def slope(a):
    return jnp.where(a > 0, 1.0, jnp.exp(jnp.minimum(a, 0.0)))


def one_utterance(x, dy, w_qkv, w_out):
    f32 = jnp.float32
    bf = jnp.bfloat16
    qkv = jnp.dot(x, w_qkv, preferred_element_type=f32).astype(bf)
    q = qkv[:, :HE].astype(f32)
    k = qkv[:, HE:2 * HE].astype(f32)
    fq = features(q).astype(bf)
    fk = features(k).astype(bf)
    v = qkv[:, 2 * HE:]
    g = jnp.dot(dy, w_out, preferred_element_type=f32).astype(bf)
    nblk = x.shape[0] // BLOCK
    shape4 = (nblk, BLOCK, HEADS, HEAD)
    fqb, fkb, vb, gb = fq.reshape(shape4), fk.reshape(shape4), v.reshape(shape4), g.reshape(shape4)
    mask = jnp.tril(jnp.ones((BLOCK, BLOCK), bool))

    def forward(carry, item_list):
        running_state, running_norm = carry
        query_feature_map, key_feature_map, value_rows, output_gradient_rows = item_list
        fq32, fk32, v32, g32 = query_feature_map.astype(f32), key_feature_map.astype(f32), value_rows.astype(f32), output_gradient_rows.astype(f32)
        block_state = running_state.astype(bf)
        scores = jnp.where(mask, jnp.einsum('thd,shd->hts', fq32, fk32), 0.0)
        den = scores.sum(-1).T + jnp.sum(fq32 * running_norm[None], -1)
        weights = scores.astype(bf).astype(f32)
        num = jnp.einsum('hts,she->the', weights, v32) + jnp.einsum('thd,hde->the', fq32, block_state.astype(f32))
        ratio = num / den[..., None]
        attention_block = ratio.astype(bf)
        numerator_gradient = (g32 / den[..., None]).astype(bf)
        denominator_gradient = -jnp.sum(g32 * ratio, -1) / den
        block_score_gradient = jnp.einsum('thd,the->hde', fq32, numerator_gradient.astype(f32))
        block_normalizer_gradient = jnp.sum(denominator_gradient[..., None] * fq32, 0)
        new = (running_state + jnp.einsum('shd,she->hde', fk32, v32), running_norm + jnp.sum(fk32, 0))
        return new, (attention_block, block_state, running_norm, numerator_gradient, denominator_gradient, block_score_gradient, block_normalizer_gradient)

    init = (jnp.zeros((HEADS, HEAD, HEAD), f32), jnp.zeros((HEADS, HEAD), f32))
    _, outs = lax.scan(forward, init, (fqb, fkb, vb, gb))
    attention_block, block_state, running_norm, numerator_gradient, denominator_gradient, block_score_gradient, block_normalizer_gradient = outs

    def backward(carry, item_list):
        dstate, dnorm = carry
        query_feature_map, key_feature_map, value_rows, sb, nz, dn, dd, dsb, dzb = item_list
        fq32, fk32, v32, dn32 = query_feature_map.astype(f32), key_feature_map.astype(f32), value_rows.astype(f32), dn.astype(f32)
        dstate_b = dstate.astype(bf).astype(f32)
        sb32 = sb.astype(f32)
        scores = jnp.where(mask, jnp.einsum('thd,shd->hts', fq32, fk32), 0.0)
        weights = scores.astype(bf).astype(f32)
        dscore = jnp.einsum('the,she->hts', dn32, v32) + dd.T[:, :, None]
        dscore = jnp.where(mask, dscore, 0.0).astype(bf).astype(f32)
        dfq = jnp.einsum('hts,shd->thd', dscore, fk32) + jnp.einsum('the,hde->thd', dn32, sb32) + dd[..., None] * nz[None]
        dfk = jnp.einsum('hts,thd->shd', dscore, fq32) + jnp.einsum('she,hde->shd', v32, dstate_b) + dnorm[None]
        dv = jnp.einsum('hts,the->she', weights, dn32) + jnp.einsum('shd,hde->she', fk32, dstate_b)
        return (dstate + dsb, dnorm + dzb), (dfq, dfk, dv)

    _, grads = lax.scan(backward, init, (fqb, fkb, vb, block_state, running_norm, numerator_gradient, denominator_gradient, block_score_gradient, block_normalizer_gradient), reverse=True)
    dfq, dfk, dv = grads
    rows = x.shape[0]
    dq = dfq.reshape(rows, HE) * slope(q)
    dk = dfk.reshape(rows, HE) * slope(k)
    dqkv = jnp.concatenate([dq, dk, dv.reshape(rows, HE)], axis=1).astype(bf)
    dx = jnp.dot(dqkv, w_qkv.T, preferred_element_type=f32).astype(bf)
    attention_block = attention_block.reshape(rows, HE)
    gq = jnp.dot(x.T, dqkv, preferred_element_type=f32)
    go = jnp.dot(dy.T, attention_block, preferred_element_type=f32)
    return dx, gq, go


def reference(frames, grad_frames, w_qkv, w_out):
    dx, gq, go = lax.map(lambda pair: one_utterance(pair[0], pair[1], w_qkv, w_out), (frames, grad_frames))
    return dx, jnp.sum(gq, 0), jnp.sum(go, 0)
```

```python
import functools

import jax
import jax.numpy as jnp
from jax import lax
from jax.experimental import pallas as pl
from jax.experimental.pallas import tpu as pltpu
from jax.sharding import PartitionSpec as P

HEADS = 12
HEAD = 64
PAIR = 128
MESH = pl.DeviceIdType.MESH
f32 = jnp.float32
bf = jnp.bfloat16


def dot(a, b, ca=1, cb=0):
    return lax.dot_general(a, b, (((ca,), (cb,)), ((), ())), preferred_element_type=f32)


def kernel(
    tm, dp, chunks,
    x_hbm, dy_hbm, wq_hbm, wo_hbm,
    dx_ref, fin_ref,
    x_ref, dy_ref, wq_ref, wo_ref,
    xf, rx, fxt,
    fq, fk, v, g, slopes,
    w_sc, a_sc, den, num, dnum, dvi, dki, ddn,
    nrm, nrm_in, st, st_in, states,
    comb, fd_in, fdb,
    gbuf, rs_in, acc,
    lsem, nsend, nrecv, ssend, srecv, xsend, xrecv, fsend, frecv, rsend, rrecv, gsend, grecv,
):
    inner = HEADS * HEAD
    pairs = inner // PAIR
    bits = tm.bit_length() - 1
    i = lax.axis_index("tm")
    d = lax.axis_index("dp")
    rows = x_ref.shape[0]
    width = x_ref.shape[1]
    block = width // tm
    cols = 4 * inner // dp
    cc = cols // chunks

    loads = [
        pltpu.make_async_copy(src, dst, lsem.at[n])
        for n, (src, dst) in enumerate(
            ((x_hbm, x_ref), (dy_hbm, dy_ref), (wq_hbm, wq_ref), (wo_hbm, wo_ref))
        )
    ]
    for copy in loads:
        copy.start()

    barrier = pltpu.get_barrier_semaphore()
    for k in range(1, tm):
        pl.semaphore_signal(
            barrier, inc=1, device_id=(lax.rem(i + k, tm), d), device_id_type=MESH
        )
    for k in range(1, dp):
        pl.semaphore_signal(
            barrier, inc=1, device_id=(i, lax.rem(d + k, dp)), device_id_type=MESH
        )

    def to_dp(k, src, dst, send, recv):
        return pltpu.make_async_remote_copy(
            src_ref=src, dst_ref=dst, send_sem=send, recv_sem=recv,
            device_id=(i, lax.rem(d + k, dp)), device_id_type=MESH,
        )

    def to_tm(peer, src, dst, send, recv):
        return pltpu.make_async_remote_copy(
            src_ref=src, dst_ref=dst, send_sem=send, recv_sem=recv,
            device_id=(peer, d), device_id_type=MESH,
        )

    sent = []

    loads[0].wait()
    loads[1].wait()
    xf[0] = x_ref[...].astype(f32)
    xf[1] = dy_ref[...].astype(f32)
    pl.semaphore_wait(barrier, tm - 1 + dp - 1)

    def second(who):
        return (who * cols) // (3 * inner)

    early = []
    for k in range(1, dp):
        peer = lax.rem(d + k, dp)
        copy = to_dp(k, xf.at[second(peer)], rx.at[k - 1], xsend.at[k - 1], xrecv.at[k - 1])
        copy.start()
        early.append(copy)
    sent += early

    lane = lax.broadcasted_iota(jnp.int32, (rows, PAIR), 1)
    lo = lane < HEAD
    lo_half = lo[:HEAD]
    tri = lax.broadcasted_iota(jnp.int32, (rows, rows), 0) >= lax.broadcasted_iota(
        jnp.int32, (rows, rows), 1
    )

    def at(p):
        return pl.ds(p * PAIR, PAIR)

    def pack(s):
        return jnp.where(lo_half, s[:HEAD], s[HEAD:])

    def unpack(s):
        zero = jnp.zeros_like(s)
        return jnp.concatenate(
            [jnp.where(lo_half, s, zero), jnp.where(lo_half, zero, s)], axis=0
        ).astype(bf)

    def keep_lo(a):
        return jnp.where(lo, a, jnp.zeros_like(a))

    def keep_hi(a):
        return jnp.where(lo, jnp.zeros_like(a), a)

    def per_head_sum(a):
        first = jnp.sum(jnp.where(lo, a, 0.0), axis=1, keepdims=True)
        both = jnp.sum(jnp.where(lo, 0.0, a), axis=1, keepdims=True)
        return jnp.where(lo, first, both)

    def features(a):
        return jnp.where(a > 0, a + 1.0, jnp.exp(jnp.minimum(a, 0.0)))

    loads[2].wait()
    x = x_ref[...]
    kk = features(dot(x, wq_ref[:, inner : 2 * inner]).astype(bf).astype(f32))
    slopes[1] = jnp.minimum(kk, 1.0)
    fk[...] = kk.astype(bf)
    v[...] = dot(x, wq_ref[:, 2 * inner :]).astype(bf)
    nrm[0] = jnp.sum(fk[...].astype(f32), axis=0, keepdims=True)

    def direct(which):
        out = []
        for k in range(1, tm):
            copy = to_tm(
                lax.rem(i + k, tm), nrm.at[which], nrm_in.at[which, k - 1],
                nsend.at[which, k - 1], nrecv.at[which, k - 1],
            )
            copy.start()
            out.append(copy)
        return out

    norm_copies = direct(0)
    sent += norm_copies

    def direct_sum(which, copies, earlier):
        total = jnp.zeros((1, inner), f32)
        for k, copy in enumerate(copies):
            copy.wait_recv()
            reached = (i - (k + 1) >= 0) if earlier else (i - (k + 1) < 0)
            total = total + jnp.where(reached, nrm_in[which, k], 0.0)
        return total

    for p in range(pairs):
        st[0, 0, pl.ds(p * HEAD, HEAD), :] = pack(dot(fk[:, at(p)], v[:, at(p)], 0, 0))

    def hop(which, b):
        peer = i + (1 << b) - 2 * (i & (1 << b))
        copy = to_tm(
            peer, st.at[which, b], st_in.at[which, b], ssend.at[which, b], srecv.at[which, b]
        )
        copy.start()
        return copy

    def last_hop():
        b = bits - 1
        bit = (i >> b) & 1
        peer = i + (1 << b) - 2 * (i & (1 << b))
        copy = to_tm(
            peer, st.at[bit, b], st_in.at[0, b], ssend.at[0, b], srecv.at[0, b]
        )
        copy.start()
        return copy

    def arrive(which, b, copy):
        copy.wait_recv()
        bit = (i >> b) & 1
        use = (bit == 1) if which == 0 else (bit == 0)
        got = st_in[which, b]
        add = jnp.where(use, got, 0.0)
        states[which] = add if b == 0 else states[which] + add
        st[which, b + 1] = st[which, b] + got

    hops = [None, None]
    hops[0] = hop(0, 0)
    sent.append(hops[0])

    qq = features(dot(x, wq_ref[:, :inner]).astype(bf).astype(f32))
    slopes[0] = jnp.minimum(qq, 1.0)
    fq[...] = qq.astype(bf)
    loads[3].wait()
    g[...] = dot(dy_ref[...], wo_ref[...]).astype(bf)

    for p in range(pairs):
        q_p, k_p, v_p = fq[:, at(p)], fk[:, at(p)], v[:, at(p)]
        s0 = jnp.where(tri, dot(keep_lo(q_p), k_p, 1, 1), 0.0)
        s1 = jnp.where(tri, dot(keep_hi(q_p), k_p, 1, 1), 0.0)
        den[:, at(p)] = jnp.where(
            lo, jnp.sum(s0, axis=1, keepdims=True), jnp.sum(s1, axis=1, keepdims=True)
        )
        w0, w1 = s0.astype(bf), s1.astype(bf)
        w_sc[2 * p] = w0
        w_sc[2 * p + 1] = w1
        num[:, at(p)] = jnp.where(lo, dot(w0, v_p), dot(w1, v_p))

    norm_in = direct_sum(0, norm_copies, True)

    for p in range(pairs):
        q_p, v_p = fq[:, at(p)], v[:, at(p)]
        total = den[:, at(p)] + per_head_sum(
            q_p.astype(f32) * norm_in[:, p * PAIR : (p + 1) * PAIR]
        )
        inverse = 1.0 / total
        den[:, at(p)] = inverse
        dn = (g[:, at(p)].astype(f32) * inverse).astype(bf)
        dnum[:, at(p)] = dn
        st[1, 0, pl.ds(p * HEAD, HEAD), :] = pack(dot(q_p, dn, 0, 0))
    hops[1] = hop(1, 0)
    sent.append(hops[1])

    for p in range(pairs):
        v_p, dn = v[:, at(p)], dnum[:, at(p)]
        a_sc[2 * p] = dot(keep_lo(dn), v_p, 1, 1)
        a_sc[2 * p + 1] = dot(keep_hi(dn), v_p, 1, 1)
        dvi[:, at(p)] = jnp.where(
            lo, dot(w_sc[2 * p], dn, 0, 0), dot(w_sc[2 * p + 1], dn, 0, 0)
        )

    for b in range(bits - 1):
        for which in (0, 1):
            arrive(which, b, hops[which])
            if b < bits - 2:
                hops[which] = hop(which, b + 1)
                sent.append(hops[which])
    last = last_hop()
    sent.append(last)

    def reverse(n):
        out = 0
        for b in range(bits):
            out = out * 2 + ((n >> b) & 1)
        return out

    def place(k, value):
        turned = value.T.astype(bf)
        for n in range(tm):
            r = reverse(n)
            fxt[n * block : (n + 1) * block, k * rows : (k + 1) * rows] = turned[
                r * block : (r + 1) * block
            ]

    place(0, xf[second(d)])
    for k in range(1, dp):
        early[k - 1].wait_recv()
        place(k, rx[k - 1])

    last.wait_recv()
    bit = (i >> (bits - 1)) & 1
    got = st_in[0, bits - 1]
    before = jnp.where(bit == 1, got, 0.0)
    after = jnp.where(bit == 0, got, 0.0)
    if bits > 1:
        before = states[0] + before
        after = states[1] + after
    states[0] = before
    states[1] = after

    for p in range(pairs):
        s_b = unpack(states[0, pl.ds(p * HEAD, HEAD), :])
        q_p = fq[:, at(p)]
        inverse = den[:, at(p)]
        ratio = (num[:, at(p)] + dot(q_p, s_b)) * inverse
        comb[:, pl.ds(3 * inner + p * PAIR, PAIR)] = ratio.astype(bf).astype(f32)
        dd = -per_head_sum(g[:, at(p)].astype(f32) * ratio) * inverse
        ddn[:, at(p)] = dd
        nrm[1, :, at(p)] = jnp.sum(dd * q_p.astype(f32), axis=0, keepdims=True)
    dnorm_copies = direct(1)
    sent += dnorm_copies

    for p in range(pairs):
        s_b = unpack(states[0, pl.ds(p * HEAD, HEAD), :])
        ds_b = unpack(states[1, pl.ds(p * HEAD, HEAD), :])
        q_p, k_p, v_p, dn, dd = fq[:, at(p)], fk[:, at(p)], v[:, at(p)], dnum[:, at(p)], ddn[:, at(p)]
        d0 = jnp.where(tri, a_sc[2 * p] + dd[:, :1], 0.0).astype(bf)
        d1 = jnp.where(tri, a_sc[2 * p + 1] + dd[:, HEAD : HEAD + 1], 0.0).astype(bf)
        dq = (
            jnp.where(lo, dot(d0, k_p), dot(d1, k_p))
            + dot(dn, s_b, 1, 1)
            + dd * norm_in[:, p * PAIR : (p + 1) * PAIR]
        )
        comb[:, at(p)] = (dq * slopes[0, :, at(p)]).astype(bf).astype(f32)
        dki[:, at(p)] = jnp.where(lo, dot(d0, q_p, 0, 0), dot(d1, q_p, 0, 0)) + dot(
            v_p, ds_b, 1, 1
        )
        dv = dvi[:, at(p)] + dot(k_p, ds_b)
        comb[:, pl.ds(2 * inner + p * PAIR, PAIR)] = dv.astype(bf).astype(f32)
    dnorm = direct_sum(1, dnorm_copies, False)
    comb[:, pl.ds(inner, inner)] = ((dki[...] + dnorm) * slopes[1]).astype(bf).astype(f32)

    factors = []
    for j in range(chunks):
        row = []
        for k in range(1, dp):
            peer = lax.rem(d + k, dp)
            start = pl.multiple_of(peer * cols + j * cc, PAIR)
            copy = to_dp(
                k, comb.at[:, pl.ds(start, cc)], fd_in.at[j, k - 1],
                fsend.at[j, k - 1], frecv.at[j, k - 1],
            )
            copy.start()
            row.append(copy)
        factors.append(row)
        sent += row

    dx_ref[...] = dot(comb[:, : 3 * inner].astype(bf), wq_ref[...], 1, 1).astype(bf)

    def halving(j, s):
        half = width >> (s + 1)
        bit = (i >> s) & 1
        peer = i + (1 << s) - 2 * (i & (1 << s))
        other = pl.multiple_of((1 - bit) * half, block)
        source = gbuf.at[j] if s == 0 else acc[s - 1].at[j]
        copy = to_tm(
            peer, source.at[pl.ds(other, half), :], rs_in[s].at[j],
            rsend.at[j, s], rrecv.at[j, s],
        )
        copy.start()
        sent.append(copy)
        return copy

    moving = {}
    for j in range(chunks):
        mine = pl.multiple_of(d * cols + j * cc, PAIR)
        fdb[0:rows, :] = comb[:, pl.ds(mine, cc)].astype(bf)
        for k in range(1, dp):
            factors[j][k - 1].wait_recv()
            fdb[k * rows : (k + 1) * rows, :] = fd_in[j, k - 1].astype(bf)
        gbuf[j] = dot(fxt[...], fdb[...])
        moving[j, 0] = halving(j, 0)

    gathers = []
    order = sorted(
        ((j, s) for j in range(chunks) for s in range(bits)), key=lambda e: 10 * e[0] + 6 * e[1]
    )
    for j, s in order:
        moving[j, s].wait_recv()
        half = width >> (s + 1)
        mine = pl.multiple_of(((i >> s) & 1) * half, block)
        source = gbuf.at[j] if s == 0 else acc[s - 1].at[j]
        acc[s][j] = source[pl.ds(mine, half), :] + rs_in[s][j]
        if s + 1 < bits:
            moving[j, s + 1] = halving(j, s + 1)
        else:
            start = pl.multiple_of(d * cols + j * cc, PAIR)
            spot = fin_ref.at[:, pl.ds(start, cc)]
            for k in range(1, dp):
                copy = to_dp(k, acc[s].at[j], spot, gsend.at[j, k - 1], grecv.at[j, k - 1])
                copy.start()
                gathers.append(copy)
            spot[...] = acc[s][j]
    sent += gathers
    for copy in gathers:
        copy.wait_recv()
    for copy in sent:
        copy.wait_send()


def per_device(tm, dp, frames, grad_frames, w_qkv, w_out):
    x, dy = frames[0], grad_frames[0]
    rows, width = x.shape
    inner = HEADS * HEAD
    cols = 4 * inner // dp
    chunks = 3
    cc = cols // chunks
    bits = tm.bit_length() - 1
    block = width // tm
    pairs = inner // PAIR
    dma = pltpu.SemaphoreType.DMA

    def vm(shape, kind=f32):
        return pltpu.VMEM(shape, kind)

    dx, fin = pl.pallas_call(
        functools.partial(kernel, tm, dp, chunks),
        out_shape=(
            jax.ShapeDtypeStruct((rows, width), bf),
            jax.ShapeDtypeStruct((block, 4 * inner), f32),
        ),
        in_specs=[pl.BlockSpec(memory_space=pl.ANY)] * 4,
        out_specs=[pl.BlockSpec(memory_space=pltpu.VMEM)] * 2,
        scratch_shapes=[
            vm((rows, width), bf), vm((rows, width), bf),
            vm(w_qkv.shape, bf), vm(w_out.shape, bf),
            vm((2, rows, width)), vm((dp - 1, rows, width)), vm((width, dp * rows), bf),
            vm((rows, inner), bf), vm((rows, inner), bf), vm((rows, inner), bf),
            vm((rows, inner), bf), vm((2, rows, inner)),
            vm((HEADS, rows, rows), bf), vm((HEADS, rows, rows)),
            vm((rows, inner)), vm((rows, inner)), vm((rows, inner), bf),
            vm((rows, inner)), vm((rows, inner)), vm((rows, inner)),
            vm((2, 1, inner)), vm((2, tm - 1, 1, inner)),
            vm((2, bits, pairs * HEAD, PAIR)), vm((2, bits, pairs * HEAD, PAIR)),
            vm((2, pairs * HEAD, PAIR)),
            vm((rows, 4 * inner)), vm((chunks, dp - 1, rows, cc)), vm((dp * rows, cc), bf),
            vm((chunks, width, cc)),
            [vm((chunks, width >> (s + 1), cc)) for s in range(bits)],
            [vm((chunks, width >> (s + 1), cc)) for s in range(bits)],
            dma((4,)),
            dma((2, tm - 1)), dma((2, tm - 1)),
            dma((2, bits)), dma((2, bits)),
            dma((dp - 1,)), dma((dp - 1,)),
            dma((chunks, dp - 1)), dma((chunks, dp - 1)),
            dma((chunks, bits)), dma((chunks, bits)),
            dma((chunks, dp - 1)), dma((chunks, dp - 1)),
        ],
        compiler_params=pltpu.CompilerParams(
            collective_id=0, has_side_effects=True, vmem_limit_bytes=60 * 1024 * 1024
        ),
    )(x, dy, w_qkv, w_out)
    return (dx[None], fin[:, : 3 * inner], fin[:, 3 * inner :])


def solution(mesh):
    placed = (P("dp", "tm", None), P("dp", "tm", None), P(), P())
    return jax.shard_map(
        functools.partial(per_device, mesh.shape["tm"], mesh.shape["dp"]),
        mesh=mesh,
        in_specs=placed,
        out_specs=(P("dp", "tm", None), P("tm", None), P("tm", None)),
        check_vma=False,
    )
```

```python
import functools

import jax
import jax.numpy as jnp
from jax import lax
from jax.experimental import pallas as pl
from jax.experimental.pallas import tpu as pltpu
from jax.sharding import PartitionSpec as P

HEADS = 12
HEAD = 64
PAIR = 128
MESH = pl.DeviceIdType.MESH
f32 = jnp.float32
bf = jnp.bfloat16


def dot(a, b, ca=1, cb=0):
    return lax.dot_general(a, b, (((ca,), (cb,)), ((), ())), preferred_element_type=f32)


def kernel(
    tm, dp, chunks,
    x_hbm, dy_hbm, wq_hbm, wo_hbm,
    dx_ref, fin_ref,
    x_ref, dy_ref, wq_ref, wo_ref,
    xf, rx, fxt,
    fq, fk, v, g, slopes,
    w_sc, a_sc, den, num, dnum, dvi, dki, ddn,
    nrm, nrm_in, st, st_in, states,
    comb, fd_in, fdb,
    gbuf, rs_in, acc,
    lsem, nsend, nrecv, ssend, srecv, xsend, xrecv, fsend, frecv, rsend, rrecv, gsend, grecv,
):
    inner = HEADS * HEAD
    pairs = inner // PAIR
    bits = tm.bit_length() - 1
    i = lax.axis_index("tm")
    d = lax.axis_index("dp")
    rows = x_ref.shape[0]
    width = x_ref.shape[1]
    block = width // tm
    cols = 4 * inner // dp
    cc = cols // chunks

    loads = [
        pltpu.make_async_copy(src, dst, lsem.at[n])
        for n, (src, dst) in enumerate(
            (
                (x_hbm, x_ref),
                (dy_hbm, dy_ref),
                (wq_hbm.at[:, pl.ds(inner, 2 * inner)], wq_ref.at[:, pl.ds(inner, 2 * inner)]),
                (wq_hbm.at[:, pl.ds(0, inner)], wq_ref.at[:, pl.ds(0, inner)]),
                (wo_hbm, wo_ref),
            )
        )
    ]
    for copy in loads:
        copy.start()

    barrier = pltpu.get_barrier_semaphore()
    for k in range(1, tm):
        pl.semaphore_signal(
            barrier, inc=1, device_id=(lax.rem(i + k, tm), d), device_id_type=MESH
        )
    for k in range(1, dp):
        pl.semaphore_signal(
            barrier, inc=1, device_id=(i, lax.rem(d + k, dp)), device_id_type=MESH
        )

    def to_dp(k, src, dst, send, recv):
        return pltpu.make_async_remote_copy(
            src_ref=src, dst_ref=dst, send_sem=send, recv_sem=recv,
            device_id=(i, lax.rem(d + k, dp)), device_id_type=MESH,
        )

    def to_tm(peer, src, dst, send, recv):
        return pltpu.make_async_remote_copy(
            src_ref=src, dst_ref=dst, send_sem=send, recv_sem=recv,
            device_id=(peer, d), device_id_type=MESH,
        )

    sent = []

    loads[0].wait()
    loads[1].wait()
    xf[0] = x_ref[...].astype(f32)
    xf[1] = dy_ref[...].astype(f32)
    pl.semaphore_wait(barrier, tm - 1 + dp - 1)

    def second(who):
        return (who * cols) // (3 * inner)

    early = []
    for k in range(1, dp):
        peer = lax.rem(d + k, dp)
        copy = to_dp(k, xf.at[second(peer)], rx.at[k - 1], xsend.at[k - 1], xrecv.at[k - 1])
        copy.start()
        early.append(copy)
    sent += early

    lane = lax.broadcasted_iota(jnp.int32, (rows, PAIR), 1)
    lo = lane < HEAD
    lo_half = lo[:HEAD]
    tri = lax.broadcasted_iota(jnp.int32, (rows, rows), 0) >= lax.broadcasted_iota(
        jnp.int32, (rows, rows), 1
    )

    def at(p):
        return pl.ds(p * PAIR, PAIR)

    def pack(s):
        return jnp.where(lo_half, s[:HEAD], s[HEAD:])

    def unpack(s):
        zero = jnp.zeros_like(s)
        return jnp.concatenate(
            [jnp.where(lo_half, s, zero), jnp.where(lo_half, zero, s)], axis=0
        ).astype(bf)

    def keep_lo(a):
        return jnp.where(lo, a, jnp.zeros_like(a))

    def keep_hi(a):
        return jnp.where(lo, jnp.zeros_like(a), a)

    def per_head_sum(a):
        first = jnp.sum(jnp.where(lo, a, 0.0), axis=1, keepdims=True)
        both = jnp.sum(jnp.where(lo, 0.0, a), axis=1, keepdims=True)
        return jnp.where(lo, first, both)

    def features(a):
        return jnp.where(a > 0, a + 1.0, jnp.exp(jnp.minimum(a, 0.0)))

    loads[2].wait()
    x = x_ref[...]
    kk = features(dot(x, wq_ref[:, inner : 2 * inner]).astype(bf).astype(f32))
    slopes[1] = jnp.minimum(kk, 1.0)
    fk[...] = kk.astype(bf)
    v[...] = dot(x, wq_ref[:, 2 * inner :]).astype(bf)
    nrm[0] = jnp.sum(fk[...].astype(f32), axis=0, keepdims=True)

    def direct(which):
        out = []
        for k in range(1, tm):
            copy = to_tm(
                lax.rem(i + k, tm), nrm.at[which], nrm_in.at[which, k - 1],
                nsend.at[which, k - 1], nrecv.at[which, k - 1],
            )
            copy.start()
            out.append(copy)
        return out

    norm_copies = direct(0)
    sent += norm_copies

    def direct_sum(which, copies, earlier):
        total = jnp.zeros((1, inner), f32)
        for k, copy in enumerate(copies):
            copy.wait_recv()
            reached = (i - (k + 1) >= 0) if earlier else (i - (k + 1) < 0)
            total = total + jnp.where(reached, nrm_in[which, k], 0.0)
        return total

    for p in range(pairs):
        st[0, 0, pl.ds(p * HEAD, HEAD), :] = pack(dot(fk[:, at(p)], v[:, at(p)], 0, 0))

    def hop(which, b):
        peer = i + (1 << b) - 2 * (i & (1 << b))
        copy = to_tm(
            peer, st.at[which, b], st_in.at[which, b], ssend.at[which, b], srecv.at[which, b]
        )
        copy.start()
        return copy

    def last_hop():
        b = bits - 1
        bit = (i >> b) & 1
        peer = i + (1 << b) - 2 * (i & (1 << b))
        copy = to_tm(
            peer, st.at[bit, b], st_in.at[0, b], ssend.at[0, b], srecv.at[0, b]
        )
        copy.start()
        return copy

    def arrive(which, b, copy):
        copy.wait_recv()
        bit = (i >> b) & 1
        use = (bit == 1) if which == 0 else (bit == 0)
        got = st_in[which, b]
        add = jnp.where(use, got, 0.0)
        states[which] = add if b == 0 else states[which] + add
        st[which, b + 1] = st[which, b] + got

    hops = [None, None]
    hops[0] = hop(0, 0)
    sent.append(hops[0])

    loads[3].wait()
    qq = features(dot(x, wq_ref[:, :inner]).astype(bf).astype(f32))
    slopes[0] = jnp.minimum(qq, 1.0)
    fq[...] = qq.astype(bf)
    loads[4].wait()
    g[...] = dot(dy_ref[...], wo_ref[...]).astype(bf)

    for p in range(pairs):
        q_p, k_p, v_p = fq[:, at(p)], fk[:, at(p)], v[:, at(p)]
        s0 = jnp.where(tri, dot(keep_lo(q_p), k_p, 1, 1), 0.0)
        s1 = jnp.where(tri, dot(keep_hi(q_p), k_p, 1, 1), 0.0)
        den[:, at(p)] = jnp.where(
            lo, jnp.sum(s0, axis=1, keepdims=True), jnp.sum(s1, axis=1, keepdims=True)
        )
        w0, w1 = s0.astype(bf), s1.astype(bf)
        w_sc[2 * p] = w0
        w_sc[2 * p + 1] = w1
        num[:, at(p)] = jnp.where(lo, dot(w0, v_p), dot(w1, v_p))

    norm_in = direct_sum(0, norm_copies, True)

    for p in range(pairs):
        q_p, v_p = fq[:, at(p)], v[:, at(p)]
        total = den[:, at(p)] + per_head_sum(
            q_p.astype(f32) * norm_in[:, p * PAIR : (p + 1) * PAIR]
        )
        inverse = 1.0 / total
        den[:, at(p)] = inverse
        dn = (g[:, at(p)].astype(f32) * inverse).astype(bf)
        dnum[:, at(p)] = dn
        st[1, 0, pl.ds(p * HEAD, HEAD), :] = pack(dot(q_p, dn, 0, 0))
    hops[1] = hop(1, 0)
    sent.append(hops[1])

    for p in range(pairs):
        v_p, dn = v[:, at(p)], dnum[:, at(p)]
        a_sc[2 * p] = dot(keep_lo(dn), v_p, 1, 1)
        a_sc[2 * p + 1] = dot(keep_hi(dn), v_p, 1, 1)
        dvi[:, at(p)] = jnp.where(
            lo, dot(w_sc[2 * p], dn, 0, 0), dot(w_sc[2 * p + 1], dn, 0, 0)
        )

    for b in range(bits - 1):
        for which in (0, 1):
            arrive(which, b, hops[which])
            if b < bits - 2:
                hops[which] = hop(which, b + 1)
                sent.append(hops[which])
    last = last_hop()
    sent.append(last)

    def reverse(n):
        out = 0
        for b in range(bits):
            out = out * 2 + ((n >> b) & 1)
        return out

    def place(k, value):
        turned = value.T.astype(bf)
        for n in range(tm):
            r = reverse(n)
            fxt[n * block : (n + 1) * block, k * rows : (k + 1) * rows] = turned[
                r * block : (r + 1) * block
            ]

    place(0, xf[second(d)])

    last.wait_recv()
    bit = (i >> (bits - 1)) & 1
    got = st_in[0, bits - 1]
    before = jnp.where(bit == 1, got, 0.0)
    after = jnp.where(bit == 0, got, 0.0)
    if bits > 1:
        before = states[0] + before
        after = states[1] + after
    states[0] = before
    states[1] = after

    for p in range(pairs):
        s_b = unpack(states[0, pl.ds(p * HEAD, HEAD), :])
        q_p = fq[:, at(p)]
        inverse = den[:, at(p)]
        ratio = (num[:, at(p)] + dot(q_p, s_b)) * inverse
        comb[:, pl.ds(3 * inner + p * PAIR, PAIR)] = ratio.astype(bf).astype(f32)
        dd = -per_head_sum(g[:, at(p)].astype(f32) * ratio) * inverse
        ddn[:, at(p)] = dd
        nrm[1, :, at(p)] = jnp.sum(dd * q_p.astype(f32), axis=0, keepdims=True)
    dnorm_copies = direct(1)
    sent += dnorm_copies

    for p in range(pairs):
        s_b = unpack(states[0, pl.ds(p * HEAD, HEAD), :])
        ds_b = unpack(states[1, pl.ds(p * HEAD, HEAD), :])
        q_p, k_p, v_p, dn, dd = fq[:, at(p)], fk[:, at(p)], v[:, at(p)], dnum[:, at(p)], ddn[:, at(p)]
        d0 = jnp.where(tri, a_sc[2 * p] + dd[:, :1], 0.0).astype(bf)
        d1 = jnp.where(tri, a_sc[2 * p + 1] + dd[:, HEAD : HEAD + 1], 0.0).astype(bf)
        dq = (
            jnp.where(lo, dot(d0, k_p), dot(d1, k_p))
            + dot(dn, s_b, 1, 1)
            + dd * norm_in[:, p * PAIR : (p + 1) * PAIR]
        )
        comb[:, at(p)] = (dq * slopes[0, :, at(p)]).astype(bf).astype(f32)
        dki[:, at(p)] = jnp.where(lo, dot(d0, q_p, 0, 0), dot(d1, q_p, 0, 0)) + dot(
            v_p, ds_b, 1, 1
        )
        dv = dvi[:, at(p)] + dot(k_p, ds_b)
        comb[:, pl.ds(2 * inner + p * PAIR, PAIR)] = dv.astype(bf).astype(f32)
    for k in range(1, dp):
        early[k - 1].wait_recv()
        place(k, rx[k - 1])
    dnorm = direct_sum(1, dnorm_copies, False)
    comb[:, pl.ds(inner, inner)] = ((dki[...] + dnorm) * slopes[1]).astype(bf).astype(f32)

    factors = []
    for j in range(chunks):
        row = []
        for k in range(1, dp):
            peer = lax.rem(d + k, dp)
            start = pl.multiple_of(peer * cols + j * cc, PAIR)
            copy = to_dp(
                k, comb.at[:, pl.ds(start, cc)], fd_in.at[j, k - 1],
                fsend.at[j, k - 1], frecv.at[j, k - 1],
            )
            copy.start()
            row.append(copy)
        factors.append(row)
        sent += row

    plain = tuple(range(bits))
    orders = [plain] * chunks
    if chunks >= 6:
        orders[1] = plain[1:] + plain[:1]

    def halving(j, s):
        half = width >> (s + 1)
        b = orders[j][s]
        bit = (i >> b) & 1
        peer = i + (1 << b) - 2 * (i & (1 << b))
        other = pl.multiple_of((1 - bit) * half, block)
        source = gbuf.at[j] if s == 0 else acc[s - 1].at[j]
        copy = to_tm(
            peer, source.at[pl.ds(other, half), :], rs_in[s].at[j],
            rsend.at[j, s], rrecv.at[j, s],
        )
        copy.start()
        sent.append(copy)
        return copy

    moving = {}
    gathers = []

    def multiply(j):
        mine = pl.multiple_of(d * cols + j * cc, PAIR)
        fdb[0:rows, :] = comb[:, pl.ds(mine, cc)].astype(bf)
        for k in range(1, dp):
            factors[j][k - 1].wait_recv()
            fdb[k * rows : (k + 1) * rows, :] = fd_in[j, k - 1].astype(bf)
        product = dot(fxt[...], fdb[...])
        if orders[j] == plain:
            gbuf[j] = product
        else:
            for n in range(tm):
                r = reverse(n)
                to = 0
                for b in orders[j]:
                    to = to * 2 + ((r >> b) & 1)
                gbuf[j, to * block : (to + 1) * block] = product[n * block : (n + 1) * block]
        moving[j, 0] = halving(j, 0)

    def reduce(j, s):
        moving[j, s].wait_recv()
        half = width >> (s + 1)
        mine = pl.multiple_of(((i >> orders[j][s]) & 1) * half, block)
        source = gbuf.at[j] if s == 0 else acc[s - 1].at[j]
        acc[s][j] = source[pl.ds(mine, half), :] + rs_in[s][j]
        if s + 1 < bits:
            moving[j, s + 1] = halving(j, s + 1)
        else:
            start = pl.multiple_of(d * cols + j * cc, PAIR)
            spot = fin_ref.at[:, pl.ds(start, cc)]
            for k in range(1, dp):
                copy = to_dp(k, acc[s].at[j], spot, gsend.at[j, k - 1], grecv.at[j, k - 1])
                copy.start()
                gathers.append(copy)
            spot[...] = acc[s][j]

    def input_gradient():
        dx_ref[...] = dot(comb[:, : 3 * inner].astype(bf), wq_ref[...], 1, 1).astype(bf)

    events = [(4.0, input_gradient, ())]
    rank = 0
    for j in range(chunks):
        events.append((2.8 * j, multiply, (j,)))
        if orders[j] == plain:
            rank += 1
            for s in range(bits):
                events.append((1.6 + 5.6 * rank + 4.5 * s, reduce, (j, s)))
        else:
            for s in range(bits):
                late = 5.6 * chunks if s == bits - 1 else 10.0 + 6.0 * s
                events.append((1.6 + late, reduce, (j, s)))
    for _, act, what in sorted(events, key=lambda e: e[0]):
        act(*what)
    sent += gathers
    for copy in gathers:
        copy.wait_recv()
    for copy in sent:
        copy.wait_send()


def per_device(tm, dp, frames, grad_frames, w_qkv, w_out):
    x, dy = frames[0], grad_frames[0]
    rows, width = x.shape
    inner = HEADS * HEAD
    cols = 4 * inner // dp
    chunks = cols // PAIR
    cc = cols // chunks
    bits = tm.bit_length() - 1
    block = width // tm
    pairs = inner // PAIR
    dma = pltpu.SemaphoreType.DMA

    def vm(shape, kind=f32):
        return pltpu.VMEM(shape, kind)

    dx, fin = pl.pallas_call(
        functools.partial(kernel, tm, dp, chunks),
        out_shape=(
            jax.ShapeDtypeStruct((rows, width), bf),
            jax.ShapeDtypeStruct((block, 4 * inner), f32),
        ),
        in_specs=[pl.BlockSpec(memory_space=pl.ANY)] * 4,
        out_specs=[pl.BlockSpec(memory_space=pltpu.VMEM)] * 2,
        scratch_shapes=[
            vm((rows, width), bf), vm((rows, width), bf),
            vm(w_qkv.shape, bf), vm(w_out.shape, bf),
            vm((2, rows, width)), vm((dp - 1, rows, width)), vm((width, dp * rows), bf),
            vm((rows, inner), bf), vm((rows, inner), bf), vm((rows, inner), bf),
            vm((rows, inner), bf), vm((2, rows, inner)),
            vm((HEADS, rows, rows), bf), vm((HEADS, rows, rows)),
            vm((rows, inner)), vm((rows, inner)), vm((rows, inner), bf),
            vm((rows, inner)), vm((rows, inner)), vm((rows, inner)),
            vm((2, 1, inner)), vm((2, tm - 1, 1, inner)),
            vm((2, bits, pairs * HEAD, PAIR)), vm((2, bits, pairs * HEAD, PAIR)),
            vm((2, pairs * HEAD, PAIR)),
            vm((rows, 4 * inner)), vm((chunks, dp - 1, rows, cc)), vm((dp * rows, cc), bf),
            vm((chunks, width, cc)),
            [vm((chunks, width >> (s + 1), cc)) for s in range(bits)],
            [vm((chunks, width >> (s + 1), cc)) for s in range(bits)],
            dma((5,)),
            dma((2, tm - 1)), dma((2, tm - 1)),
            dma((2, bits)), dma((2, bits)),
            dma((dp - 1,)), dma((dp - 1,)),
            dma((chunks, dp - 1)), dma((chunks, dp - 1)),
            dma((chunks, bits)), dma((chunks, bits)),
            dma((chunks, dp - 1)), dma((chunks, dp - 1)),
        ],
        compiler_params=pltpu.CompilerParams(
            collective_id=0, has_side_effects=True, vmem_limit_bytes=60 * 1024 * 1024
        ),
    )(x, dy, w_qkv, w_out)
    return (dx[None], fin[:, : 3 * inner], fin[:, 3 * inner :])


def solution(mesh):
    placed = (P("dp", "tm", None), P("dp", "tm", None), P(), P())
    return jax.shard_map(
        functools.partial(per_device, mesh.shape["tm"], mesh.shape["dp"]),
        mesh=mesh,
        in_specs=placed,
        out_specs=(P("dp", "tm", None), P("tm", None), P("tm", None)),
        check_vma=False,
    )
```

```python
import functools

import jax
import jax.numpy as jnp
from jax import lax
from jax.experimental import pallas as pl
from jax.experimental.pallas import tpu as pltpu
from jax.sharding import PartitionSpec as P

HEADS = 12
HEAD = 64
PAIR = 128
MESH = pl.DeviceIdType.MESH
f32 = jnp.float32
bf = jnp.bfloat16


def dot(a, b, ca=1, cb=0):
    return lax.dot_general(a, b, (((ca,), (cb,)), ((), ())), preferred_element_type=f32)


def kernel(
    tm, dp, chunks,
    x_hbm, dy_hbm, wq_hbm, wo_hbm,
    dx_ref, fin_ref,
    x_ref, dy_ref, wq_ref, wo_ref,
    xf, rx, fxt,
    fq, fk, v, g, slopes,
    w_sc, a_sc, den, num, dnum, dvi, dki, ddn,
    nrm, nrm_in, st, st_in, states,
    comb, fd_in, fdb,
    gbuf, rs_in, acc,
    lsem, nsend, nrecv, ssend, srecv, xsend, xrecv, fsend, frecv, rsend, rrecv, gsend, grecv,
):
    inner = HEADS * HEAD
    pairs = inner // PAIR
    bits = tm.bit_length() - 1
    i = lax.axis_index("tm")
    d = lax.axis_index("dp")
    rows = x_ref.shape[0]
    width = x_ref.shape[1]
    block = width // tm
    cols = 4 * inner // dp
    cc = cols // chunks

    loads = [
        pltpu.make_async_copy(src, dst, lsem.at[n])
        for n, (src, dst) in enumerate(
            (
                (x_hbm, x_ref),
                (dy_hbm, dy_ref),
                (wq_hbm.at[:, pl.ds(inner, 2 * inner)], wq_ref.at[:, pl.ds(inner, 2 * inner)]),
                (wq_hbm.at[:, pl.ds(0, inner)], wq_ref.at[:, pl.ds(0, inner)]),
                (wo_hbm, wo_ref),
            )
        )
    ]
    for copy in loads:
        copy.start()

    barrier = pltpu.get_barrier_semaphore()
    for k in range(1, tm):
        pl.semaphore_signal(
            barrier, inc=1, device_id=(lax.rem(i + k, tm), d), device_id_type=MESH
        )
    for k in range(1, dp):
        pl.semaphore_signal(
            barrier, inc=1, device_id=(i, lax.rem(d + k, dp)), device_id_type=MESH
        )

    def to_dp(k, src, dst, send, recv):
        return pltpu.make_async_remote_copy(
            src_ref=src, dst_ref=dst, send_sem=send, recv_sem=recv,
            device_id=(i, lax.rem(d + k, dp)), device_id_type=MESH,
        )

    def to_tm(peer, src, dst, send, recv):
        return pltpu.make_async_remote_copy(
            src_ref=src, dst_ref=dst, send_sem=send, recv_sem=recv,
            device_id=(peer, d), device_id_type=MESH,
        )

    sent = []

    loads[0].wait()
    loads[1].wait()
    xf[0] = x_ref[...].astype(f32)
    xf[1] = dy_ref[...].astype(f32)
    pl.semaphore_wait(barrier, tm - 1 + dp - 1)

    def second(who):
        return (who * cols) // (3 * inner)

    early = []
    for k in range(1, dp):
        peer = lax.rem(d + k, dp)
        copy = to_dp(k, xf.at[second(peer)], rx.at[k - 1], xsend.at[k - 1], xrecv.at[k - 1])
        copy.start()
        early.append(copy)
    sent += early

    lane = lax.broadcasted_iota(jnp.int32, (rows, PAIR), 1)
    lo = lane < HEAD
    lo_half = lo[:HEAD]
    tri = lax.broadcasted_iota(jnp.int32, (rows, rows), 0) >= lax.broadcasted_iota(
        jnp.int32, (rows, rows), 1
    )

    def at(p):
        return pl.ds(p * PAIR, PAIR)

    def pack(s):
        return jnp.where(lo_half, s[:HEAD], s[HEAD:])

    def unpack(s):
        zero = jnp.zeros_like(s)
        return jnp.concatenate(
            [jnp.where(lo_half, s, zero), jnp.where(lo_half, zero, s)], axis=0
        ).astype(bf)

    def keep_lo(a):
        return jnp.where(lo, a, jnp.zeros_like(a))

    def keep_hi(a):
        return jnp.where(lo, jnp.zeros_like(a), a)

    def per_head_sum(a):
        first = jnp.sum(jnp.where(lo, a, 0.0), axis=1, keepdims=True)
        both = jnp.sum(jnp.where(lo, 0.0, a), axis=1, keepdims=True)
        return jnp.where(lo, first, both)

    def features(a):
        return jnp.where(a > 0, a + 1.0, jnp.exp(jnp.minimum(a, 0.0)))

    loads[2].wait()
    x = x_ref[...]
    kk = features(dot(x, wq_ref[:, inner : 2 * inner]).astype(bf).astype(f32))
    slopes[1] = jnp.minimum(kk, 1.0)
    fk[...] = kk.astype(bf)
    v[...] = dot(x, wq_ref[:, 2 * inner :]).astype(bf)
    nrm[0] = jnp.sum(fk[...].astype(f32), axis=0, keepdims=True)

    def direct(which):
        out = []
        for k in range(1, tm):
            copy = to_tm(
                lax.rem(i + k, tm), nrm.at[which], nrm_in.at[which, k - 1],
                nsend.at[which, k - 1], nrecv.at[which, k - 1],
            )
            copy.start()
            out.append(copy)
        return out

    norm_copies = direct(0)
    sent += norm_copies

    def direct_sum(which, copies, earlier):
        total = jnp.zeros((1, inner), f32)
        for k, copy in enumerate(copies):
            copy.wait_recv()
            reached = (i - (k + 1) >= 0) if earlier else (i - (k + 1) < 0)
            total = total + jnp.where(reached, nrm_in[which, k], 0.0)
        return total

    def part(p):
        return pl.ds(p * HEAD, HEAD)

    def exchange(which, b, p, slot):
        peer = i + (1 << b) - 2 * (i & (1 << b))
        copy = to_tm(
            peer, st.at[which, b, part(p)], st_in.at[slot, b, part(p)],
            ssend.at[slot, b, p], srecv.at[slot, b, p],
        )
        copy.start()
        sent.append(copy)
        hops[slot, b, p] = copy

    def hop(which, b, p):
        if b < bits - 1:
            exchange(which, b, p, which)
        elif which == 1:
            exchange((i >> b) & 1, b, p, 0)

    def arrive(which, b, p):
        hops[which, b, p].wait_recv()
        bit = (i >> b) & 1
        use = (bit == 1) if which == 0 else (bit == 0)
        got = st_in[which, b, part(p)]
        add = jnp.where(use, got, 0.0)
        states[which, part(p)] = add if b == 0 else states[which, part(p)] + add
        st[which, b + 1, part(p)] = st[which, b, part(p)] + got
        hop(which, b + 1, p)

    hops = {}
    for p in range(pairs):
        st[0, 0, part(p)] = pack(dot(fk[:, at(p)], v[:, at(p)], 0, 0))
        hop(0, 0, p)

    loads[3].wait()
    qq = features(dot(x, wq_ref[:, :inner]).astype(bf).astype(f32))
    slopes[0] = jnp.minimum(qq, 1.0)
    fq[...] = qq.astype(bf)
    loads[4].wait()
    g[...] = dot(dy_ref[...], wo_ref[...]).astype(bf)

    for p in range(pairs):
        q_p, k_p, v_p = fq[:, at(p)], fk[:, at(p)], v[:, at(p)]
        s0 = jnp.where(tri, dot(keep_lo(q_p), k_p, 1, 1), 0.0)
        s1 = jnp.where(tri, dot(keep_hi(q_p), k_p, 1, 1), 0.0)
        den[:, at(p)] = jnp.where(
            lo, jnp.sum(s0, axis=1, keepdims=True), jnp.sum(s1, axis=1, keepdims=True)
        )
        w0, w1 = s0.astype(bf), s1.astype(bf)
        w_sc[2 * p] = w0
        w_sc[2 * p + 1] = w1
        num[:, at(p)] = jnp.where(lo, dot(w0, v_p), dot(w1, v_p))

    if bits > 1:
        for p in range(pairs):
            arrive(0, 0, p)
    norm_in = direct_sum(0, norm_copies, True)

    for p in range(pairs):
        q_p, v_p = fq[:, at(p)], v[:, at(p)]
        total = den[:, at(p)] + per_head_sum(
            q_p.astype(f32) * norm_in[:, p * PAIR : (p + 1) * PAIR]
        )
        inverse = 1.0 / total
        den[:, at(p)] = inverse
        dn = (g[:, at(p)].astype(f32) * inverse).astype(bf)
        dnum[:, at(p)] = dn
        st[1, 0, part(p)] = pack(dot(q_p, dn, 0, 0))
        hop(1, 0, p)

    for p in range(pairs):
        v_p, dn = v[:, at(p)], dnum[:, at(p)]
        a_sc[2 * p] = dot(keep_lo(dn), v_p, 1, 1)
        a_sc[2 * p + 1] = dot(keep_hi(dn), v_p, 1, 1)
        dvi[:, at(p)] = jnp.where(
            lo, dot(w_sc[2 * p], dn, 0, 0), dot(w_sc[2 * p + 1], dn, 0, 0)
        )

    waits = [
        (4.0 * which + 0.7 * p + 2.4 * b, which, b, p)
        for which in (0, 1)
        for b in range(1 - which, bits - 1)
        for p in range(pairs)
    ]
    for _, which, b, p in sorted(waits):
        arrive(which, b, p)

    def reverse(n):
        out = 0
        for b in range(bits):
            out = out * 2 + ((n >> b) & 1)
        return out

    def place(k, value):
        turned = value.T.astype(bf)
        for n in range(tm):
            r = reverse(n)
            fxt[n * block : (n + 1) * block, k * rows : (k + 1) * rows] = turned[
                r * block : (r + 1) * block
            ]

    place(0, xf[second(d)])

    top = (i >> (bits - 1)) & 1

    def settle(p):
        hops[0, bits - 1, p].wait_recv()
        got = st_in[0, bits - 1, part(p)]
        before = jnp.where(top == 1, got, 0.0)
        after = jnp.where(top == 0, got, 0.0)
        if bits > 1:
            before = states[0, part(p)] + before
            after = states[1, part(p)] + after
        states[0, part(p)] = before
        states[1, part(p)] = after

    for p in range(pairs):
        settle(p)
        s_b = unpack(states[0, part(p)])
        q_p = fq[:, at(p)]
        inverse = den[:, at(p)]
        ratio = (num[:, at(p)] + dot(q_p, s_b)) * inverse
        comb[:, pl.ds(3 * inner + p * PAIR, PAIR)] = ratio.astype(bf).astype(f32)
        dd = -per_head_sum(g[:, at(p)].astype(f32) * ratio) * inverse
        ddn[:, at(p)] = dd
        nrm[1, :, at(p)] = jnp.sum(dd * q_p.astype(f32), axis=0, keepdims=True)
    dnorm_copies = direct(1)
    sent += dnorm_copies

    for p in range(pairs):
        s_b = unpack(states[0, pl.ds(p * HEAD, HEAD), :])
        ds_b = unpack(states[1, pl.ds(p * HEAD, HEAD), :])
        q_p, k_p, v_p, dn, dd = fq[:, at(p)], fk[:, at(p)], v[:, at(p)], dnum[:, at(p)], ddn[:, at(p)]
        d0 = jnp.where(tri, a_sc[2 * p] + dd[:, :1], 0.0).astype(bf)
        d1 = jnp.where(tri, a_sc[2 * p + 1] + dd[:, HEAD : HEAD + 1], 0.0).astype(bf)
        dq = (
            jnp.where(lo, dot(d0, k_p), dot(d1, k_p))
            + dot(dn, s_b, 1, 1)
            + dd * norm_in[:, p * PAIR : (p + 1) * PAIR]
        )
        comb[:, at(p)] = (dq * slopes[0, :, at(p)]).astype(bf).astype(f32)
        dki[:, at(p)] = jnp.where(lo, dot(d0, q_p, 0, 0), dot(d1, q_p, 0, 0)) + dot(
            v_p, ds_b, 1, 1
        )
        dv = dvi[:, at(p)] + dot(k_p, ds_b)
        comb[:, pl.ds(2 * inner + p * PAIR, PAIR)] = dv.astype(bf).astype(f32)
    for k in range(1, dp):
        early[k - 1].wait_recv()
        place(k, rx[k - 1])
    dnorm = direct_sum(1, dnorm_copies, False)
    comb[:, pl.ds(inner, inner)] = ((dki[...] + dnorm) * slopes[1]).astype(bf).astype(f32)

    factors = []
    for j in range(chunks):
        row = []
        for k in range(1, dp):
            peer = lax.rem(d + k, dp)
            start = pl.multiple_of(peer * cols + j * cc, PAIR)
            copy = to_dp(
                k, comb.at[:, pl.ds(start, cc)], fd_in.at[j, k - 1],
                fsend.at[j, k - 1], frecv.at[j, k - 1],
            )
            copy.start()
            row.append(copy)
        factors.append(row)
        sent += row

    plain = tuple(range(bits))
    orders = [plain] * chunks
    if chunks >= 6:
        orders[1] = plain[1:] + plain[:1]

    def halving(j, s):
        half = width >> (s + 1)
        b = orders[j][s]
        bit = (i >> b) & 1
        peer = i + (1 << b) - 2 * (i & (1 << b))
        other = pl.multiple_of((1 - bit) * half, block)
        source = gbuf.at[j] if s == 0 else acc[s - 1].at[j]
        copy = to_tm(
            peer, source.at[pl.ds(other, half), :], rs_in[s].at[j],
            rsend.at[j, s], rrecv.at[j, s],
        )
        copy.start()
        sent.append(copy)
        return copy

    moving = {}
    gathers = []

    def multiply(j):
        mine = pl.multiple_of(d * cols + j * cc, PAIR)
        fdb[0:rows, :] = comb[:, pl.ds(mine, cc)].astype(bf)
        for k in range(1, dp):
            factors[j][k - 1].wait_recv()
            fdb[k * rows : (k + 1) * rows, :] = fd_in[j, k - 1].astype(bf)
        product = dot(fxt[...], fdb[...])
        if orders[j] == plain:
            gbuf[j] = product
        else:
            for n in range(tm):
                r = reverse(n)
                to = 0
                for b in orders[j]:
                    to = to * 2 + ((r >> b) & 1)
                gbuf[j, to * block : (to + 1) * block] = product[n * block : (n + 1) * block]
        moving[j, 0] = halving(j, 0)

    def reduce(j, s):
        moving[j, s].wait_recv()
        half = width >> (s + 1)
        mine = pl.multiple_of(((i >> orders[j][s]) & 1) * half, block)
        source = gbuf.at[j] if s == 0 else acc[s - 1].at[j]
        acc[s][j] = source[pl.ds(mine, half), :] + rs_in[s][j]
        if s + 1 < bits:
            moving[j, s + 1] = halving(j, s + 1)
        else:
            start = pl.multiple_of(d * cols + j * cc, PAIR)
            spot = fin_ref.at[:, pl.ds(start, cc)]
            for k in range(1, dp):
                copy = to_dp(k, acc[s].at[j], spot, gsend.at[j, k - 1], grecv.at[j, k - 1])
                copy.start()
                gathers.append(copy)
            spot[...] = acc[s][j]

    def input_gradient():
        dx_ref[...] = dot(comb[:, : 3 * inner].astype(bf), wq_ref[...], 1, 1).astype(bf)

    events = [(4.0, input_gradient, ())]
    rank = 0
    for j in range(chunks):
        events.append((2.8 * j, multiply, (j,)))
        if orders[j] == plain:
            rank += 1
            for s in range(bits):
                events.append((1.6 + 5.6 * rank + 4.5 * s, reduce, (j, s)))
        else:
            for s in range(bits):
                late = 5.6 * chunks if s == bits - 1 else 10.0 + 6.0 * s
                events.append((1.6 + late, reduce, (j, s)))
    for _, act, what in sorted(events, key=lambda e: e[0]):
        act(*what)
    sent += gathers
    for copy in gathers:
        copy.wait_recv()
    for copy in sent:
        copy.wait_send()


def per_device(tm, dp, frames, grad_frames, w_qkv, w_out):
    x, dy = frames[0], grad_frames[0]
    rows, width = x.shape
    inner = HEADS * HEAD
    cols = 4 * inner // dp
    chunks = cols // PAIR
    cc = cols // chunks
    bits = tm.bit_length() - 1
    block = width // tm
    pairs = inner // PAIR
    dma = pltpu.SemaphoreType.DMA

    def vm(shape, kind=f32):
        return pltpu.VMEM(shape, kind)

    dx, fin = pl.pallas_call(
        functools.partial(kernel, tm, dp, chunks),
        out_shape=(
            jax.ShapeDtypeStruct((rows, width), bf),
            jax.ShapeDtypeStruct((block, 4 * inner), f32),
        ),
        in_specs=[pl.BlockSpec(memory_space=pl.ANY)] * 4,
        out_specs=[pl.BlockSpec(memory_space=pltpu.VMEM)] * 2,
        scratch_shapes=[
            vm((rows, width), bf), vm((rows, width), bf),
            vm(w_qkv.shape, bf), vm(w_out.shape, bf),
            vm((2, rows, width)), vm((dp - 1, rows, width)), vm((width, dp * rows), bf),
            vm((rows, inner), bf), vm((rows, inner), bf), vm((rows, inner), bf),
            vm((rows, inner), bf), vm((2, rows, inner)),
            vm((HEADS, rows, rows), bf), vm((HEADS, rows, rows)),
            vm((rows, inner)), vm((rows, inner)), vm((rows, inner), bf),
            vm((rows, inner)), vm((rows, inner)), vm((rows, inner)),
            vm((2, 1, inner)), vm((2, tm - 1, 1, inner)),
            vm((2, bits, pairs * HEAD, PAIR)), vm((2, bits, pairs * HEAD, PAIR)),
            vm((2, pairs * HEAD, PAIR)),
            vm((rows, 4 * inner)), vm((chunks, dp - 1, rows, cc)), vm((dp * rows, cc), bf),
            vm((chunks, width, cc)),
            [vm((chunks, width >> (s + 1), cc)) for s in range(bits)],
            [vm((chunks, width >> (s + 1), cc)) for s in range(bits)],
            dma((5,)),
            dma((2, tm - 1)), dma((2, tm - 1)),
            dma((2, bits, pairs)), dma((2, bits, pairs)),
            dma((dp - 1,)), dma((dp - 1,)),
            dma((chunks, dp - 1)), dma((chunks, dp - 1)),
            dma((chunks, bits)), dma((chunks, bits)),
            dma((chunks, dp - 1)), dma((chunks, dp - 1)),
        ],
        compiler_params=pltpu.CompilerParams(
            collective_id=0, has_side_effects=True, vmem_limit_bytes=60 * 1024 * 1024
        ),
    )(x, dy, w_qkv, w_out)
    return (dx[None], fin[:, : 3 * inner], fin[:, 3 * inner :])


def solution(mesh):
    placed = (P("dp", "tm", None), P("dp", "tm", None), P(), P())
    return jax.shard_map(
        functools.partial(per_device, mesh.shape["tm"], mesh.shape["dp"]),
        mesh=mesh,
        in_specs=placed,
        out_specs=(P("dp", "tm", None), P("tm", None), P("tm", None)),
        check_vma=False,
    )
```
